32 devices in a mesh: ctx: 4 (over y, core), head: 2 (over x), dp: 4 (over z).
Axes of the slice: x: 2, y: 2, z: 4, core: 2. Of those that a mesh axis runs over, the one named last changes fastest.
Arguments:
- queries: bfloat16 [1024, 6144], P(('dp', 'ctx', 'head')), parts along dimension 0, may hold values from -18 to 18
- keys: bfloat16 [1024, 1024], P(('dp', 'ctx', 'head')), parts along dimension 0, may hold values from -9 to 9
- values: bfloat16 [1024, 1024], P(('dp', 'ctx', 'head')), parts along dimension 0, may hold values from -6 to 6
- level_gain: float32 [64, 6144], P(None, 'head'), may hold values from 0.5 to 4
- levels: int32 [16], P('dp'), parts along dimension 0, may hold values from 0 to 63
- visible: int32 [16, 4], P('dp'), parts along dimension 0, may hold values from 0 to 1, as said below
- counts: int32 [16], P('dp'), parts along dimension 0, may hold values from 32 to 64, as said below
Outputs:
- mixed: bfloat16 [1024, 6144], P(('dp', 'ctx', 'head')), parts along dimension 0
- finished: bfloat16 [256, 6144], P(('dp', 'ctx'), 'head'), parts along dimension 0
The draws below stay inside these ranges and needn't reach their ends.
There are 4 independent parts, one for each index of `dp`. The reference program is written for one: setup_inputs(seed, part) draws one part's arguments, and reference() takes and returns one part's arrays. A program takes and returns all parts, laid end to end along the dimension named above; an argument that names none is the same for every part. Nothing has to cross between parts.
Inputs may be any that keep to these rules, and one draw needn't show every extreme that they name: visible[c][c] is 1, visible[c][d] is 0 for d > c, and entries below the diagonal are 0 or 1. `counts`: every clip has at least half of its slots live, and in every draw some clip has all 64 live.
All inputs are finite; a program needn't handle non-finite values.
Results may differ from the reference program's by a relative error of at most 0.0045.
Values may be sent and summed in bfloat16 or wider, within the bound.
No kernel may reach another device: no remote copies, remote signals or barrier semaphores. Data moves between devices by JAX's collectives and lax.ppermute only.
A program may use at most 64 MiB of HBM per device.

```python
import math
import jax
import jax.numpy as jnp
from jax import lax

QUERY_HEADS = 48
KEY_VALUE_HEADS = 8
HEAD_SIZE = 128
LEVELS = 64
CLIPS = 4
ALL_CLIP_TOKENS = 256
CLIP_TOK = 64


def paired_draw(key):
    query_key = jax.random.fold_in(key, 11)
    key_random_seed = jax.random.fold_in(key, 12)
    query_draw = jnp.clip(1.4 * jax.random.normal(query_key, (ALL_CLIP_TOKENS, QUERY_HEADS * HEAD_SIZE), jnp.float32), -8.4, 8.4)
    sampled_keys = jnp.clip(1.4 * jax.random.normal(key_random_seed, (ALL_CLIP_TOKENS, KEY_VALUE_HEADS * HEAD_SIZE), jnp.float32), -8.4, 8.4)
    return (query_draw, sampled_keys)


def draw_queries(key, part):
    return paired_draw(key)[0].astype(jnp.bfloat16)


def draw_keys(key, part):
    return paired_draw(key)[1].astype(jnp.bfloat16)


def draw_visible(key, part):
    random_bits = jax.random.randint(jax.random.fold_in(key, 31), (CLIPS, CLIPS), 0, 2, dtype=jnp.int32)
    row_index = jnp.arange(CLIPS, dtype=jnp.int32)[:, None]
    column_index = jnp.arange(CLIPS, dtype=jnp.int32)[None, :]
    lower_part = jnp.where(column_index < row_index, random_bits, 0)
    return jnp.where(row_index == column_index, 1, lower_part).astype(jnp.int32)


def draw_counts(key, part):
    random_counts = jax.random.randint(jax.random.fold_in(key, 21), (CLIPS,), CLIP_TOK // 2, CLIP_TOK + 1, dtype=jnp.int32)
    full_clip = jax.random.randint(jax.random.fold_in(key, 22), (), 0, CLIPS, dtype=jnp.int32)
    return jnp.where(jnp.arange(CLIPS, dtype=jnp.int32) == full_clip, CLIP_TOK, random_counts).astype(jnp.int32)


def touch_ends(array, key, smallest, largest):
    index_at = [jax.random.randint(jax.random.fold_in(key, axis), (), 0, length) for axis, length in enumerate(array.shape)]
    longest = array.shape.index(max(array.shape))
    neighbour = index_at[:longest] + [(index_at[longest] + 1) % array.shape[longest]] + index_at[longest + 1:]
    return array.at[tuple(index_at)].set(smallest).at[tuple(neighbour)].set(largest)


def block_scale(key, extent, cuts, low, high):
    level = 1.0
    for position, shards_of in cuts:
        steps = jax.random.uniform(jax.random.fold_in(jax.random.fold_in(key, 6), position), (shards_of,), jnp.float32, low / len(cuts), high / len(cuts))
        level = level * jnp.repeat(jnp.exp(steps), extent[position] // shards_of).reshape((-1,) + (1,) * (len(extent) - 1 - position))
    return level


def scatter_about(rng, shape, width, bound, pieces=(), held_as=jnp.bfloat16):
    result = jax.random.normal(rng, shape, jnp.float32) * width
    if len(pieces) > 0:
        result = block_scale(rng, shape, pieces, -0.22, 0.18) * result
    return jnp.clip(result, min=-bound, max=bound).astype(held_as)


def setup_inputs(seed: int = 0, part: int = 0) -> dict:
    key_list = jax.random.split(jax.random.key(seed), 8)
    part_splits = jax.random.split(jax.random.fold_in(key_list[7], part), 8)
    queries = draw_queries(jax.random.fold_in(jax.random.fold_in(key_list[7], part), 71), part)
    keys = draw_keys(jax.random.fold_in(jax.random.fold_in(key_list[7], part), 71), part)
    values = scatter_about(part_splits[2], (ALL_CLIP_TOKENS, KEY_VALUE_HEADS * HEAD_SIZE), 1.0, 6.0, ((0, 8),))
    level_gain = jnp.clip(jnp.exp(math.log(4.0) - 2.0794415 * jax.random.uniform(key_list[3], (LEVELS, QUERY_HEADS * HEAD_SIZE), jnp.float32) ** block_scale(key_list[3], (LEVELS, QUERY_HEADS * HEAD_SIZE), ((1, 2),), -0.2, 0.2)), 0.5, 4.0)
    levels = touch_ends(jax.random.randint(part_splits[4], (CLIPS,), 0, LEVELS), jax.random.fold_in(part_splits[4], 1), 0, LEVELS - 1).astype(jnp.int32)
    visible = draw_visible(jax.random.fold_in(jax.random.fold_in(key_list[7], part), 71), part)
    counts = draw_counts(jax.random.fold_in(jax.random.fold_in(key_list[7], part), 71), part)
    return dict(queries=queries, keys=keys, values=values, level_gain=level_gain, levels=levels, visible=visible, counts=counts)


def reference(queries, keys, values, level_gain, levels, visible, counts):
    token_ids = jnp.arange(ALL_CLIP_TOKENS, dtype=jnp.int32)
    clip_ids = token_ids // CLIP_TOK
    live_rows = token_ids % CLIP_TOK < counts[clip_ids]
    allowed = (visible[clip_ids][:, clip_ids] == 1) & live_rows[None, :]
    heads_per_group = QUERY_HEADS // KEY_VALUE_HEADS
    query_heads = queries.reshape(ALL_CLIP_TOKENS, QUERY_HEADS, HEAD_SIZE).transpose(1, 0, 2)
    key_head_rows = keys.reshape(ALL_CLIP_TOKENS, KEY_VALUE_HEADS, HEAD_SIZE).transpose(1, 0, 2)
    value_head_rows = values.reshape(ALL_CLIP_TOKENS, KEY_VALUE_HEADS, HEAD_SIZE).transpose(1, 0, 2)
    scale = 1.0 / math.sqrt(HEAD_SIZE)

    def per_head(head_index):
        query_head = query_heads[head_index]
        key_head = key_head_rows[head_index // heads_per_group]
        value_head = value_head_rows[head_index // heads_per_group]
        scores = jnp.dot(query_head, key_head.T, preferred_element_type=jnp.float32) * scale
        scores = jnp.where(allowed, scores, -1e+30)
        row_peak = lax.optimization_barrier(jnp.max(scores, axis=1, keepdims=True))
        probs = jnp.where(allowed, jnp.exp(scores - row_peak), 0.0)
        denominator = lax.optimization_barrier(jnp.sum(probs, axis=1, keepdims=True))
        weighted = jnp.dot(probs.astype(jnp.bfloat16), value_head, preferred_element_type=jnp.float32)
        return weighted / denominator
    attended = lax.map(per_head, jnp.arange(QUERY_HEADS, dtype=jnp.int32))
    attended = attended.transpose(1, 0, 2).reshape(ALL_CLIP_TOKENS, QUERY_HEADS * HEAD_SIZE)
    gate_rows = level_gain[levels[clip_ids]]
    mixed = jnp.where(live_rows[:, None], attended * gate_rows, 0.0).astype(jnp.bfloat16)
    return (mixed, mixed[:CLIP_TOK])
```

```python
import functools
import math

import jax
import jax.numpy as jnp
from jax import lax
from jax.experimental import pallas as pl
from jax.experimental.pallas import tpu as pltpu
from jax.sharding import PartitionSpec as P

QUERY_HEADS = 48
KEY_VALUE_HEADS = 8
HEAD_SIZE = 128
LEVELS = 64
CLIPS = 4


def from_behind(block, axis, distance):
    devices = range(lax.axis_size(axis))
    route = [(i - distance, i) for i in devices if i - distance in devices]
    return lax.ppermute(block, axis, route)


def general_body(queries, keys, values, level_gain, levels, visible, counts):
    head_count = lax.axis_size("head")
    ctx_count = lax.axis_size("ctx")
    ctx_index = lax.axis_index("ctx")
    tok_rows = queries.shape[0]
    rows_ctx = tok_rows * head_count
    clip_tok = rows_ctx * ctx_count // CLIPS
    heads_per_group = QUERY_HEADS // KEY_VALUE_HEADS
    scale = 1.0 / math.sqrt(HEAD_SIZE)
    clip_range = jnp.arange(CLIPS, dtype=jnp.int32)
    source_count = ctx_count // CLIPS
    query_local, key_local, value_local = (
        lax.all_to_all(queries, "head", split_axis=1, concat_axis=0, tiled=True),
        lax.all_to_all(keys, "head", split_axis=1, concat_axis=0, tiled=True),
        lax.all_to_all(values, "head", split_axis=1, concat_axis=0, tiled=True),
    )
    query_width = query_local.shape[1]
    query_ids = ctx_index * rows_ctx + jnp.arange(rows_ctx, dtype=jnp.int32)
    row_groups = [(0, rows_ctx)]
    query_grouped = query_local.reshape(rows_ctx, -1, heads_per_group, HEAD_SIZE)
    local_kv_heads = query_grouped.shape[1]
    query_onehot = (query_ids // clip_tok)[:, None] == clip_range[None, :]
    query_count = jnp.sum(jnp.where(query_onehot, counts[None, :], 0), axis=1)
    query_live = query_ids % clip_tok < query_count
    query_sees = jnp.sum(jnp.where(query_onehot[:, :, None], visible[None, :, :], 0), axis=1) == 1
    query_level = jnp.sum(jnp.where(query_onehot, levels[None, :], 0), axis=1)

    def key_block(carry_state, key_block_rows, value_block_rows, first_row):
        block_rows = key_block_rows.shape[0]
        key_ids = first_row + jnp.arange(block_rows, dtype=jnp.int32)
        key_onehot = (key_ids // clip_tok)[:, None] == clip_range[None, :]
        key_count = jnp.sum(jnp.where(key_onehot, counts[None, :], 0), axis=1)
        key_live = key_ids % clip_tok < key_count
        block_clips = jnp.any(key_onehot & key_live[:, None], axis=0)
        key_head_rows = key_block_rows.reshape(block_rows, -1, HEAD_SIZE)
        value_head_rows = value_block_rows.reshape(block_rows, -1, HEAD_SIZE)
        group_start, group_rows = row_groups[0]
        group_end = group_start + group_rows
        part_state = tuple((member for member in carry_state))
        group_sees = query_sees
        needed = jnp.any(jnp.any(group_sees, axis=0) & block_clips)

        def update(state, group_sees=group_sees, group_start=group_start, group_end=group_end):
            running_max, denominator, weighted = state
            allowed = (
                jnp.any(group_sees[:, None, :] & key_onehot[None, :, :], axis=-1)
                & key_live[None, :]
            )
            scores = (
                jnp.einsum(
                    "rkgd,nkd->rkgn",
                    query_grouped,
                    key_head_rows,
                    preferred_element_type=jnp.float32,
                )
                * scale
            )
            key_mask = allowed[:, None, None, :]
            scores = jnp.where(key_mask, scores, -1e30)
            new_max = jnp.maximum(running_max, jnp.max(scores, axis=-1))
            weights = jnp.where(key_mask, jnp.exp(scores - new_max[..., None]), 0.0)
            shrink = jnp.exp(running_max - new_max)
            denominator = denominator * shrink + jnp.sum(weights, axis=-1)
            weighted = weighted * shrink[..., None] + jnp.einsum(
                "rkgn,nkd->rkgd",
                weights.astype(jnp.bfloat16),
                value_head_rows,
                preferred_element_type=jnp.float32,
            )
            return (new_max, denominator, weighted)

        def keep(state):
            return state

        group_states = [lax.cond(needed, update, keep, part_state)]
        if len(group_states) == 1:
            return group_states[0]
        return tuple(
            (
                jnp.concatenate([state[member] for state in group_states], axis=0)
                for member in range(3)
            )
        )

    initial = (
        jnp.full((rows_ctx, local_kv_heads, heads_per_group), -1e30, jnp.float32),
        jnp.zeros((rows_ctx, local_kv_heads, heads_per_group), jnp.float32),
        jnp.zeros((rows_ctx, local_kv_heads, heads_per_group, HEAD_SIZE), jnp.float32),
    )
    key_piece = lax.all_gather(key_local, "ctx", axis=0, tiled=True)
    value_piece = lax.all_gather(value_local, "ctx", axis=0, tiled=True)
    piece_rows = key_piece.shape[0]
    block_rows = math.gcd(piece_rows, 512)

    def advance(block_index, inner_state):
        key_slice = lax.dynamic_slice_in_dim(key_piece, block_index * block_rows, block_rows, 0)
        value_slice = lax.dynamic_slice_in_dim(value_piece, block_index * block_rows, block_rows, 0)
        return key_block(inner_state, key_slice, value_slice, block_index * block_rows)

    final_state = lax.fori_loop(0, piece_rows // block_rows, advance, initial)
    attended = (final_state[2] / final_state[1][..., None]).reshape(rows_ctx, query_width)
    level_onehot = (query_level[:, None] == jnp.arange(LEVELS, dtype=jnp.int32)[None, :]).astype(
        jnp.float32
    )
    gate_rows = jnp.dot(
        level_onehot,
        level_gain,
        precision=lax.Precision.HIGHEST,
        preferred_element_type=jnp.float32,
    )
    gated = jnp.where(query_live[:, None], attended * gate_rows, 0.0).astype(jnp.bfloat16)
    mixed = lax.all_to_all(gated, "head", split_axis=0, concat_axis=1, tiled=True)
    relay_rows = rows_ctx // CLIPS
    held = jnp.where(ctx_index < source_count, gated, jnp.zeros_like(gated)).reshape(
        CLIPS, relay_rows, query_width
    )
    empty_block = jnp.zeros_like(held)
    sources = jnp.arange(source_count, dtype=jnp.int32)
    hop_bits = (source_count - 1).bit_length()
    for bit_number in reversed(range(hop_bits)):
        higher = sources >> bit_number + 1 << bit_number + 1
        places = sources + 3 * higher
        holds_bit = jnp.any((places == ctx_index) & (sources >> bit_number & 1 == 1))
        moving = jnp.where(holds_bit, held, empty_block)
        staying = jnp.where(holds_bit, empty_block, held)
        arriving = from_behind(moving, "ctx", 3 * (1 << bit_number))
        held = staying + arriving
    group_position = ctx_index % CLIPS
    finished = held[0]
    for lane_number in range(1, CLIPS):
        arriving_tile = from_behind(held[lane_number], "ctx", lane_number)
        finished = jnp.where(group_position == lane_number, arriving_tile, finished)
    return (mixed, finished)


def attention_kernel(
    counts_ref,
    visible_ref,
    query_ref,
    first_refs,
    key_refs,
    value_refs,
    gain_ref,
    far_gain_ref,
    first_gain_ref,
    mixed_ref,
    finished_ref,
):
    ctx, head = lax.axis_index("ctx"), lax.axis_index("head")
    rows, width = query_ref.shape
    half = width // 2
    first_rows = finished_ref.shape[0]
    group = QUERY_HEADS // KEY_VALUE_HEADS
    group_width = group * HEAD_SIZE
    pieces = len(key_refs)
    key_count = pieces * rows
    scale = 1.0 / math.sqrt(HEAD_SIZE)

    lane = lax.broadcasted_iota(jnp.int32, (1, key_count), 1)
    piece = lane // rows
    place = jnp.where(piece % 2 == head, 0, rows) + lane % rows
    bias = jnp.full((1, key_count), -1e30, jnp.float32)
    first_bias = bias
    for flip in range(pieces // 2):
        clip = ctx ^ ((flip % 2) * 2) ^ (flip // 2)
        here = (piece // 2 == flip) & (place < counts_ref[clip])
        seen = jnp.where(visible_ref[ctx, clip] == 1, 0.0, -1e30)
        bias = jnp.where(here, seen, bias)
        first_bias = jnp.where(here, jnp.where(clip == 0, 0.0, -1e30), first_bias)

    def attend(query_pieces, keys, values, key_bias):
        stacked = jnp.concatenate(query_pieces, axis=0)
        scores = lax.dot_general(
            stacked, keys, (((1,), (1,)), ((), ())), preferred_element_type=jnp.float32
        )
        scores = scores * scale + key_bias
        peak = jnp.max(scores, axis=1, keepdims=True)
        probs = jnp.exp(scores - peak)
        denominator = jnp.sum(probs, axis=1, keepdims=True)
        weighted = jnp.dot(
            probs.astype(jnp.bfloat16), values, preferred_element_type=jnp.float32
        )
        return weighted / denominator

    row = lax.broadcasted_iota(jnp.int32, (rows, 1), 0)
    live = row + head * rows < counts_ref[ctx]
    for kv_head in range(KEY_VALUE_HEADS):
        columns = slice(kv_head * HEAD_SIZE, (kv_head + 1) * HEAD_SIZE)
        keys = jnp.concatenate([ref[:, columns] for ref in key_refs], axis=0)
        values = jnp.concatenate([ref[:, columns] for ref in value_refs], axis=0)
        start = kv_head * group_width
        spans = [slice(start + g * HEAD_SIZE, start + (g + 1) * HEAD_SIZE) for g in range(group)]
        attended = attend([query_ref[:, span] for span in spans], keys, values, bias)
        for g, span in enumerate(spans):
            side = span.start // half
            local = slice(span.start - side * half, span.stop - side * half)
            gain = jnp.where(head == side, gain_ref[:, local], far_gain_ref[:, local])
            block = attended[g * rows : (g + 1) * rows] * gain
            mixed_ref[:, span] = jnp.where(live, block, 0.0).astype(mixed_ref.dtype)

    first_row = lax.broadcasted_iota(jnp.int32, (first_rows, 1), 0)
    first_live = first_row + ctx * first_rows < counts_ref[0]
    lower, upper = first_rows * (ctx % 2), half * head
    for kv_head in range(KEY_VALUE_HEADS // 2):
        start = pl.multiple_of((head * (KEY_VALUE_HEADS // 2) + kv_head) * HEAD_SIZE, HEAD_SIZE)
        columns = pl.ds(start, HEAD_SIZE)
        keys = jnp.concatenate([ref[:, columns] for ref in key_refs], axis=0)
        values = jnp.concatenate([ref[:, columns] for ref in value_refs], axis=0)
        start = kv_head * group_width
        spans = [slice(start + g * HEAD_SIZE, start + (g + 1) * HEAD_SIZE) for g in range(group)]
        query_pieces = []
        for span in spans:
            near, near_other, far, far_other = [ref[:, span] for ref in first_refs]
            own = query_ref[:first_rows, span]
            even = jnp.where(head == 1, near, jnp.where(ctx == 0, own, far))
            odd = jnp.where(head == 1, near_other, far_other)
            query_pieces.append(jnp.where(ctx % 2 == 0, even, odd))
        attended = attend(query_pieces, keys, values, first_bias)
        for g, span in enumerate(spans):
            block = attended[g * first_rows : (g + 1) * first_rows] * first_gain_ref[:, span]
            finished_ref[:, span] = jnp.where(first_live, block, 0.0).astype(finished_ref.dtype)


def paired_body(queries, keys, values, level_gain, levels, visible, counts):
    axes = ("ctx", "head")
    places = [(c, h) for c in range(CLIPS) for h in range(2)]
    ctx = lax.axis_index("ctx")
    rows, width = queries.shape
    half = width // 2
    first_rows = rows * 2 // CLIPS

    def move(block, route):
        pairs = [(a * 2 + b, c * 2 + d) for (a, b), (c, d) in route]
        return lax.ppermute(block, axes, pairs)

    beside = [((c, h), (c, 1 - h)) for c, h in places]
    across = [((c, h), (c ^ 2, h)) for c, h in places]
    relay = [((c, h), (c, 1 - h)) for c, h in places if c >= 2]
    partner = [((c, h), (c ^ 1, h)) for c, h in places]
    across_keys, across_values = move(keys, across), move(values, across)
    beside_keys, beside_values = move(keys, beside), move(values, beside)
    relay_keys, relay_values = move(across_keys, relay), move(across_values, relay)
    near_keys = [keys, beside_keys, across_keys, relay_keys]
    near_values = [values, beside_values, across_values, relay_values]
    all_keys = near_keys + [move(block, partner) for block in near_keys]
    all_values = near_values + [move(block, partner) for block in near_values]

    upper, lower = queries[:first_rows], queries[first_rows:]
    first_queries = [
        move(upper[:, half:], [((0, 0), (0, 1)), ((0, 1), (2, 1))]),
        move(lower[:, half:], [((0, 0), (1, 1)), ((0, 1), (3, 1))]),
        move(upper[:, :half], [((0, 1), (2, 0))]),
        move(lower[:, :half], [((0, 0), (1, 0)), ((0, 1), (3, 0))]),
    ]
    gain = lax.dynamic_slice_in_dim(level_gain, levels[ctx], 1, 0)
    first_gain = lax.dynamic_slice_in_dim(level_gain, levels[0], 1, 0)
    far_gain = move(gain, beside)
    smem, vmem = pl.BlockSpec(memory_space=pltpu.SMEM), pl.BlockSpec(memory_space=pltpu.VMEM)
    pieces = len(all_keys)
    return pl.pallas_call(
        attention_kernel,
        out_shape=(
            jax.ShapeDtypeStruct((rows, width), queries.dtype),
            jax.ShapeDtypeStruct((first_rows, half), queries.dtype),
        ),
        in_specs=[smem, smem, vmem, [vmem] * 4, [vmem] * pieces, [vmem] * pieces, vmem, vmem, vmem],
        out_specs=(vmem, vmem),
        name="attention",
    )(counts, visible, queries, first_queries, all_keys, all_values, gain, far_gain, first_gain)


def solution(mesh):
    placed = (
        P(("dp", "ctx", "head"), None),
        P(("dp", "ctx", "head"), None),
        P(("dp", "ctx", "head"), None),
        P(None, "head"),
        P("dp"),
        P("dp", None),
        P("dp"),
    )
    axes = mesh.shape
    small = axes["ctx"] == CLIPS and axes["head"] == 2
    return jax.shard_map(
        paired_body if small else general_body,
        mesh=mesh,
        in_specs=placed,
        out_specs=(P(("dp", "ctx", "head"), None), P(("dp", "ctx"), "head")),
        check_vma=False,
    )
```

```python
import math

import jax
import jax.numpy as jnp
from jax import lax
from jax.experimental import pallas as pl
from jax.experimental.pallas import tpu as pltpu
from jax.sharding import PartitionSpec as P

QUERY_HEADS = 48
KEY_VALUE_HEADS = 8
HEAD_SIZE = 128
LEVELS = 64
CLIPS = 4


def from_behind(block, axis, distance):
    devices = range(lax.axis_size(axis))
    route = [(i - distance, i) for i in devices if i - distance in devices]
    return lax.ppermute(block, axis, route)


def general_body(queries, keys, values, level_gain, levels, visible, counts):
    head_count = lax.axis_size("head")
    ctx_count = lax.axis_size("ctx")
    ctx_index = lax.axis_index("ctx")
    tok_rows = queries.shape[0]
    rows_ctx = tok_rows * head_count
    clip_tok = rows_ctx * ctx_count // CLIPS
    heads_per_group = QUERY_HEADS // KEY_VALUE_HEADS
    scale = 1.0 / math.sqrt(HEAD_SIZE)
    clip_range = jnp.arange(CLIPS, dtype=jnp.int32)
    source_count = ctx_count // CLIPS
    query_local, key_local, value_local = (
        lax.all_to_all(queries, "head", split_axis=1, concat_axis=0, tiled=True),
        lax.all_to_all(keys, "head", split_axis=1, concat_axis=0, tiled=True),
        lax.all_to_all(values, "head", split_axis=1, concat_axis=0, tiled=True),
    )
    query_width = query_local.shape[1]
    query_ids = ctx_index * rows_ctx + jnp.arange(rows_ctx, dtype=jnp.int32)
    row_groups = [(0, rows_ctx)]
    query_grouped = query_local.reshape(rows_ctx, -1, heads_per_group, HEAD_SIZE)
    local_kv_heads = query_grouped.shape[1]
    query_onehot = (query_ids // clip_tok)[:, None] == clip_range[None, :]
    query_count = jnp.sum(jnp.where(query_onehot, counts[None, :], 0), axis=1)
    query_live = query_ids % clip_tok < query_count
    query_sees = jnp.sum(jnp.where(query_onehot[:, :, None], visible[None, :, :], 0), axis=1) == 1
    query_level = jnp.sum(jnp.where(query_onehot, levels[None, :], 0), axis=1)

    def key_block(carry_state, key_block_rows, value_block_rows, first_row):
        block_rows = key_block_rows.shape[0]
        key_ids = first_row + jnp.arange(block_rows, dtype=jnp.int32)
        key_onehot = (key_ids // clip_tok)[:, None] == clip_range[None, :]
        key_count = jnp.sum(jnp.where(key_onehot, counts[None, :], 0), axis=1)
        key_live = key_ids % clip_tok < key_count
        block_clips = jnp.any(key_onehot & key_live[:, None], axis=0)
        key_head_rows = key_block_rows.reshape(block_rows, -1, HEAD_SIZE)
        value_head_rows = value_block_rows.reshape(block_rows, -1, HEAD_SIZE)
        group_start, group_rows = row_groups[0]
        group_end = group_start + group_rows
        part_state = tuple((member for member in carry_state))
        group_sees = query_sees
        needed = jnp.any(jnp.any(group_sees, axis=0) & block_clips)

        def update(state, group_sees=group_sees, group_start=group_start, group_end=group_end):
            running_max, denominator, weighted = state
            allowed = (
                jnp.any(group_sees[:, None, :] & key_onehot[None, :, :], axis=-1)
                & key_live[None, :]
            )
            scores = (
                jnp.einsum(
                    "rkgd,nkd->rkgn",
                    query_grouped,
                    key_head_rows,
                    preferred_element_type=jnp.float32,
                )
                * scale
            )
            key_mask = allowed[:, None, None, :]
            scores = jnp.where(key_mask, scores, -1e30)
            new_max = jnp.maximum(running_max, jnp.max(scores, axis=-1))
            weights = jnp.where(key_mask, jnp.exp(scores - new_max[..., None]), 0.0)
            shrink = jnp.exp(running_max - new_max)
            denominator = denominator * shrink + jnp.sum(weights, axis=-1)
            weighted = weighted * shrink[..., None] + jnp.einsum(
                "rkgn,nkd->rkgd",
                weights.astype(jnp.bfloat16),
                value_head_rows,
                preferred_element_type=jnp.float32,
            )
            return (new_max, denominator, weighted)

        def keep(state):
            return state

        group_states = [lax.cond(needed, update, keep, part_state)]
        if len(group_states) == 1:
            return group_states[0]
        return tuple(
            (
                jnp.concatenate([state[member] for state in group_states], axis=0)
                for member in range(3)
            )
        )

    initial = (
        jnp.full((rows_ctx, local_kv_heads, heads_per_group), -1e30, jnp.float32),
        jnp.zeros((rows_ctx, local_kv_heads, heads_per_group), jnp.float32),
        jnp.zeros((rows_ctx, local_kv_heads, heads_per_group, HEAD_SIZE), jnp.float32),
    )
    key_piece = lax.all_gather(key_local, "ctx", axis=0, tiled=True)
    value_piece = lax.all_gather(value_local, "ctx", axis=0, tiled=True)
    piece_rows = key_piece.shape[0]
    block_rows = math.gcd(piece_rows, 512)

    def advance(block_index, inner_state):
        key_slice = lax.dynamic_slice_in_dim(key_piece, block_index * block_rows, block_rows, 0)
        value_slice = lax.dynamic_slice_in_dim(value_piece, block_index * block_rows, block_rows, 0)
        return key_block(inner_state, key_slice, value_slice, block_index * block_rows)

    final_state = lax.fori_loop(0, piece_rows // block_rows, advance, initial)
    attended = (final_state[2] / final_state[1][..., None]).reshape(rows_ctx, query_width)
    level_onehot = (query_level[:, None] == jnp.arange(LEVELS, dtype=jnp.int32)[None, :]).astype(
        jnp.float32
    )
    gate_rows = jnp.dot(
        level_onehot,
        level_gain,
        precision=lax.Precision.HIGHEST,
        preferred_element_type=jnp.float32,
    )
    gated = jnp.where(query_live[:, None], attended * gate_rows, 0.0).astype(jnp.bfloat16)
    mixed = lax.all_to_all(gated, "head", split_axis=0, concat_axis=1, tiled=True)
    relay_rows = rows_ctx // CLIPS
    held = jnp.where(ctx_index < source_count, gated, jnp.zeros_like(gated)).reshape(
        CLIPS, relay_rows, query_width
    )
    empty_block = jnp.zeros_like(held)
    sources = jnp.arange(source_count, dtype=jnp.int32)
    hop_bits = (source_count - 1).bit_length()
    for bit_number in reversed(range(hop_bits)):
        higher = sources >> bit_number + 1 << bit_number + 1
        places = sources + 3 * higher
        holds_bit = jnp.any((places == ctx_index) & (sources >> bit_number & 1 == 1))
        moving = jnp.where(holds_bit, held, empty_block)
        staying = jnp.where(holds_bit, empty_block, held)
        arriving = from_behind(moving, "ctx", 3 * (1 << bit_number))
        held = staying + arriving
    group_position = ctx_index % CLIPS
    finished = held[0]
    for lane_number in range(1, CLIPS):
        arriving_tile = from_behind(held[lane_number], "ctx", lane_number)
        finished = jnp.where(group_position == lane_number, arriving_tile, finished)
    return (mixed, finished)


KERNEL_BYTES = 8 << 20


def prepare_kernel(levels_ref, visible_ref, counts_ref, gain_ref, gains_ref, bias_ref, live_ref):
    ctx, head = lax.axis_index("ctx"), lax.axis_index("head")
    for place, clip in enumerate((ctx, 0)):
        gains_ref[pl.ds(place, 1)] = gain_ref[pl.ds(levels_ref[clip], 1)]
    key_count = bias_ref.shape[1]
    rows = live_ref.shape[1]
    first_rows = rows * 2 // CLIPS

    lane = lax.broadcasted_iota(jnp.int32, (1, key_count), 1)
    piece = lane // rows
    place = jnp.where(piece % 2 == head, 0, rows) + lane % rows
    bias = jnp.full((1, key_count), -1e30, jnp.float32)
    first_bias = bias
    for flip in range(CLIPS):
        clip = ctx ^ ((flip % 2) * 2) ^ (flip // 2)
        here = (piece // 2 == flip) & (place < counts_ref[clip])
        seen = jnp.where(visible_ref[ctx, clip] == 1, 0.0, -1e30)
        bias = jnp.where(here, seen, bias)
        first_bias = jnp.where(here, jnp.where(clip == 0, 0.0, -1e30), first_bias)
    bias_ref[:1] = bias
    bias_ref[1:] = first_bias
    row = lax.broadcasted_iota(jnp.int32, live_ref.shape[1:], 0)
    live_ref[0] = jnp.where(row + head * rows < counts_ref[ctx], 1.0, 0.0)
    live_ref[1] = jnp.where(row + ctx * first_rows < counts_ref[0], 1.0, 0.0)


def attend(query_pieces, keys, values, key_bias):
    scale = 1.0 / math.sqrt(HEAD_SIZE)
    stacked = jnp.concatenate(query_pieces, axis=0)
    scores = lax.dot_general(
        stacked, keys, (((1,), (1,)), ((), ())), preferred_element_type=jnp.float32
    )
    scores = scores * scale + key_bias
    peak = jnp.max(scores, axis=1, keepdims=True)
    probs = jnp.exp(scores - peak)
    denominator = jnp.sum(probs, axis=1, keepdims=True)
    weighted = jnp.dot(probs.astype(jnp.bfloat16), values, preferred_element_type=jnp.float32)
    return weighted / denominator


def attention_kernel(query_ref, key_refs, value_refs, bias_ref, live_ref, gain_ref, far_gain_ref, mixed_ref):
    head = lax.axis_index("head")
    rows, width = query_ref.shape
    half = width // 2
    group = QUERY_HEADS // KEY_VALUE_HEADS
    live = live_ref[0] != 0.0
    for kv_head in range(KEY_VALUE_HEADS):
        columns = slice(kv_head * HEAD_SIZE, (kv_head + 1) * HEAD_SIZE)
        keys = jnp.concatenate([ref[:, columns] for ref in key_refs], axis=0)
        values = jnp.concatenate([ref[:, columns] for ref in value_refs], axis=0)
        start = kv_head * group * HEAD_SIZE
        spans = [slice(start + g * HEAD_SIZE, start + (g + 1) * HEAD_SIZE) for g in range(group)]
        attended = attend([query_ref[:, span] for span in spans], keys, values, bias_ref[:1])
        for g, span in enumerate(spans):
            side = span.start // half
            local = slice(span.start - side * half, span.stop - side * half)
            gain = jnp.where(head == side, gain_ref[:1, local], far_gain_ref[:1, local])
            block = attended[g * rows : (g + 1) * rows] * gain
            mixed_ref[:, span] = jnp.where(live, block, 0.0).astype(mixed_ref.dtype)


def first_kernel(query_refs, key_refs, value_refs, bias_ref, live_ref, gain_ref, finished_ref):
    ctx, head = lax.axis_index("ctx"), lax.axis_index("head")
    kept_ref, beside_ref, across_ref = query_refs
    rows = finished_ref.shape[0]
    group = QUERY_HEADS // KEY_VALUE_HEADS
    live = live_ref[1, :rows] != 0.0
    for kv_head in range(KEY_VALUE_HEADS // 2):
        start = pl.multiple_of((head * (KEY_VALUE_HEADS // 2) + kv_head) * HEAD_SIZE, HEAD_SIZE)
        columns = pl.ds(start, HEAD_SIZE)
        keys = jnp.concatenate([ref[:, columns] for ref in key_refs], axis=0)
        values = jnp.concatenate([ref[:, columns] for ref in value_refs], axis=0)
        start = kv_head * group * HEAD_SIZE
        spans = [slice(start + g * HEAD_SIZE, start + (g + 1) * HEAD_SIZE) for g in range(group)]
        query_pieces = [
            jnp.where(
                ctx < 2,
                jnp.where(head == 0, kept_ref[:, span], beside_ref[:, span]),
                across_ref[:, span],
            )
            for span in spans
        ]
        attended = attend(query_pieces, keys, values, bias_ref[1:])
        for g, span in enumerate(spans):
            block = attended[g * rows : (g + 1) * rows] * gain_ref[1:, span]
            finished_ref[:, span] = jnp.where(live, block, 0.0).astype(finished_ref.dtype)


def paired_body(queries, keys, values, level_gain, levels, visible, counts):
    axes = ("ctx", "head")
    places = [(c, h) for c in range(CLIPS) for h in range(2)]
    ctx, head = lax.axis_index("ctx"), lax.axis_index("head")
    rows, width = queries.shape
    half = width // 2
    first_rows = rows * 2 // CLIPS

    def move(block, route):
        pairs = [(a * 2 + b, c * 2 + d) for (a, b), (c, d) in route]
        return lax.ppermute(block, axes, pairs)

    beside = [((c, h), (c, 1 - h)) for c, h in places]
    across = [((c, h), (c ^ 2, h)) for c, h in places]
    partner = [((c, h), (c ^ 1, h)) for c, h in places]
    smem, vmem = pl.BlockSpec(memory_space=pltpu.SMEM), pl.BlockSpec(memory_space=pltpu.VMEM)
    params = pltpu.CompilerParams(vmem_limit_bytes=KERNEL_BYTES)
    swapped = move(queries, partner)
    beside_keys, beside_values = move(keys, beside), move(values, beside)
    across_keys, across_values = move(keys, across), move(values, across)
    relay_keys, relay_values = move(beside_keys, across), move(beside_values, across)
    near_keys = [keys, beside_keys, across_keys, relay_keys]
    near_values = [values, beside_values, across_values, relay_values]
    all_keys = near_keys + [move(b, partner) for b in near_keys]
    all_values = near_values + [move(b, partner) for b in near_values]

    mine = jnp.where(ctx % 2 == 0, queries[:first_rows], swapped[first_rows:])
    left, right = mine[:, :half], mine[:, half:]
    sent, kept = jnp.where(head == 0, right, left), jnp.where(head == 0, left, right)
    first_beside = move(sent, beside)
    onward = jnp.where(head == 1, kept, first_beside)
    first_across = move(onward, across)

    gains, bias, live = pl.pallas_call(
        prepare_kernel,
        out_shape=(
            jax.ShapeDtypeStruct((2, half), level_gain.dtype),
            jax.ShapeDtypeStruct((2, len(all_keys) * rows), jnp.float32),
            jax.ShapeDtypeStruct((2, rows, HEAD_SIZE), jnp.float32),
        ),
        in_specs=[smem, smem, smem, vmem],
        out_specs=(vmem, vmem, vmem),
        compiler_params=params,
        name="prepare",
    )(levels, visible, counts, level_gain)
    far_gains = move(gains, beside)
    pieces = [vmem] * len(all_keys)
    mixed = pl.pallas_call(
        attention_kernel,
        out_shape=jax.ShapeDtypeStruct((rows, width), queries.dtype),
        in_specs=[vmem, pieces, pieces, vmem, vmem, vmem, vmem],
        out_specs=vmem,
        compiler_params=params,
        name="attention",
    )(queries, all_keys, all_values, bias, live, gains, far_gains)
    finished = pl.pallas_call(
        first_kernel,
        out_shape=jax.ShapeDtypeStruct((first_rows, half), queries.dtype),
        in_specs=[[vmem] * 3, pieces, pieces, vmem, vmem, vmem],
        out_specs=vmem,
        compiler_params=params,
        name="first_clip",
    )([kept, first_beside, first_across], all_keys, all_values, bias, live, gains)
    return mixed, finished


def solution(mesh):
    placed = (
        P(("dp", "ctx", "head"), None),
        P(("dp", "ctx", "head"), None),
        P(("dp", "ctx", "head"), None),
        P(None, "head"),
        P("dp"),
        P("dp", None),
        P("dp"),
    )
    axes = mesh.shape
    paired = axes["ctx"] == CLIPS and axes["head"] == 2
    return jax.shard_map(
        paired_body if paired else general_body,
        mesh=mesh,
        in_specs=placed,
        out_specs=(P(("dp", "ctx", "head"), None), P(("dp", "ctx"), "head")),
        check_vma=False,
    )
```

```python
import math

import jax
import jax.numpy as jnp
from jax import lax
from jax.experimental import pallas as pl
from jax.experimental.pallas import tpu as pltpu
from jax.sharding import PartitionSpec as P

QUERY_HEADS = 48
KEY_VALUE_HEADS = 8
HEAD_SIZE = 128
LEVELS = 64
CLIPS = 4


def from_behind(block, axis, distance):
    devices = range(lax.axis_size(axis))
    route = [(i - distance, i) for i in devices if i - distance in devices]
    return lax.ppermute(block, axis, route)


def general_body(queries, keys, values, level_gain, levels, visible, counts):
    head_count = lax.axis_size("head")
    ctx_count = lax.axis_size("ctx")
    ctx_index = lax.axis_index("ctx")
    tok_rows = queries.shape[0]
    rows_ctx = tok_rows * head_count
    clip_tok = rows_ctx * ctx_count // CLIPS
    heads_per_group = QUERY_HEADS // KEY_VALUE_HEADS
    scale = 1.0 / math.sqrt(HEAD_SIZE)
    clip_range = jnp.arange(CLIPS, dtype=jnp.int32)
    source_count = ctx_count // CLIPS
    query_local, key_local, value_local = (
        lax.all_to_all(queries, "head", split_axis=1, concat_axis=0, tiled=True),
        lax.all_to_all(keys, "head", split_axis=1, concat_axis=0, tiled=True),
        lax.all_to_all(values, "head", split_axis=1, concat_axis=0, tiled=True),
    )
    query_width = query_local.shape[1]
    query_ids = ctx_index * rows_ctx + jnp.arange(rows_ctx, dtype=jnp.int32)
    row_groups = [(0, rows_ctx)]
    query_grouped = query_local.reshape(rows_ctx, -1, heads_per_group, HEAD_SIZE)
    local_kv_heads = query_grouped.shape[1]
    query_onehot = (query_ids // clip_tok)[:, None] == clip_range[None, :]
    query_count = jnp.sum(jnp.where(query_onehot, counts[None, :], 0), axis=1)
    query_live = query_ids % clip_tok < query_count
    query_sees = jnp.sum(jnp.where(query_onehot[:, :, None], visible[None, :, :], 0), axis=1) == 1
    query_level = jnp.sum(jnp.where(query_onehot, levels[None, :], 0), axis=1)

    def key_block(carry_state, key_block_rows, value_block_rows, first_row):
        block_rows = key_block_rows.shape[0]
        key_ids = first_row + jnp.arange(block_rows, dtype=jnp.int32)
        key_onehot = (key_ids // clip_tok)[:, None] == clip_range[None, :]
        key_count = jnp.sum(jnp.where(key_onehot, counts[None, :], 0), axis=1)
        key_live = key_ids % clip_tok < key_count
        block_clips = jnp.any(key_onehot & key_live[:, None], axis=0)
        key_head_rows = key_block_rows.reshape(block_rows, -1, HEAD_SIZE)
        value_head_rows = value_block_rows.reshape(block_rows, -1, HEAD_SIZE)
        group_start, group_rows = row_groups[0]
        group_end = group_start + group_rows
        part_state = tuple((member for member in carry_state))
        group_sees = query_sees
        needed = jnp.any(jnp.any(group_sees, axis=0) & block_clips)

        def update(state, group_sees=group_sees, group_start=group_start, group_end=group_end):
            running_max, denominator, weighted = state
            allowed = (
                jnp.any(group_sees[:, None, :] & key_onehot[None, :, :], axis=-1)
                & key_live[None, :]
            )
            scores = (
                jnp.einsum(
                    "rkgd,nkd->rkgn",
                    query_grouped,
                    key_head_rows,
                    preferred_element_type=jnp.float32,
                )
                * scale
            )
            key_mask = allowed[:, None, None, :]
            scores = jnp.where(key_mask, scores, -1e30)
            new_max = jnp.maximum(running_max, jnp.max(scores, axis=-1))
            weights = jnp.where(key_mask, jnp.exp(scores - new_max[..., None]), 0.0)
            shrink = jnp.exp(running_max - new_max)
            denominator = denominator * shrink + jnp.sum(weights, axis=-1)
            weighted = weighted * shrink[..., None] + jnp.einsum(
                "rkgn,nkd->rkgd",
                weights.astype(jnp.bfloat16),
                value_head_rows,
                preferred_element_type=jnp.float32,
            )
            return (new_max, denominator, weighted)

        def keep(state):
            return state

        group_states = [lax.cond(needed, update, keep, part_state)]
        if len(group_states) == 1:
            return group_states[0]
        return tuple(
            (
                jnp.concatenate([state[member] for state in group_states], axis=0)
                for member in range(3)
            )
        )

    initial = (
        jnp.full((rows_ctx, local_kv_heads, heads_per_group), -1e30, jnp.float32),
        jnp.zeros((rows_ctx, local_kv_heads, heads_per_group), jnp.float32),
        jnp.zeros((rows_ctx, local_kv_heads, heads_per_group, HEAD_SIZE), jnp.float32),
    )
    key_piece = lax.all_gather(key_local, "ctx", axis=0, tiled=True)
    value_piece = lax.all_gather(value_local, "ctx", axis=0, tiled=True)
    piece_rows = key_piece.shape[0]
    block_rows = math.gcd(piece_rows, 512)

    def advance(block_index, inner_state):
        key_slice = lax.dynamic_slice_in_dim(key_piece, block_index * block_rows, block_rows, 0)
        value_slice = lax.dynamic_slice_in_dim(value_piece, block_index * block_rows, block_rows, 0)
        return key_block(inner_state, key_slice, value_slice, block_index * block_rows)

    final_state = lax.fori_loop(0, piece_rows // block_rows, advance, initial)
    attended = (final_state[2] / final_state[1][..., None]).reshape(rows_ctx, query_width)
    level_onehot = (query_level[:, None] == jnp.arange(LEVELS, dtype=jnp.int32)[None, :]).astype(
        jnp.float32
    )
    gate_rows = jnp.dot(
        level_onehot,
        level_gain,
        precision=lax.Precision.HIGHEST,
        preferred_element_type=jnp.float32,
    )
    gated = jnp.where(query_live[:, None], attended * gate_rows, 0.0).astype(jnp.bfloat16)
    mixed = lax.all_to_all(gated, "head", split_axis=0, concat_axis=1, tiled=True)
    relay_rows = rows_ctx // CLIPS
    held = jnp.where(ctx_index < source_count, gated, jnp.zeros_like(gated)).reshape(
        CLIPS, relay_rows, query_width
    )
    empty_block = jnp.zeros_like(held)
    sources = jnp.arange(source_count, dtype=jnp.int32)
    hop_bits = (source_count - 1).bit_length()
    for bit_number in reversed(range(hop_bits)):
        higher = sources >> bit_number + 1 << bit_number + 1
        places = sources + 3 * higher
        holds_bit = jnp.any((places == ctx_index) & (sources >> bit_number & 1 == 1))
        moving = jnp.where(holds_bit, held, empty_block)
        staying = jnp.where(holds_bit, empty_block, held)
        arriving = from_behind(moving, "ctx", 3 * (1 << bit_number))
        held = staying + arriving
    group_position = ctx_index % CLIPS
    finished = held[0]
    for lane_number in range(1, CLIPS):
        arriving_tile = from_behind(held[lane_number], "ctx", lane_number)
        finished = jnp.where(group_position == lane_number, arriving_tile, finished)
    return (mixed, finished)


KERNEL_BYTES = 8 << 20


def prepare_kernel(levels_ref, visible_ref, counts_ref, gain_ref, gains_ref, bias_ref, live_ref):
    ctx, head = lax.axis_index("ctx"), lax.axis_index("head")
    key_count, rows = bias_ref.shape[1], live_ref.shape[1]
    first_rows = rows * 2 // CLIPS

    def pick_out(ref, index):
        picked = jnp.zeros((1, 1), ref.dtype)
        for clip in range(CLIPS):
            picked = jnp.where(index == clip, ref[:, clip : clip + 1], picked)
        return picked

    level_rows = lax.broadcasted_iota(jnp.int32, (gain_ref.shape[0], 1), 0)
    for place, clip in enumerate((ctx, 0)):
        chosen = jnp.where(level_rows == pick_out(levels_ref, clip), gain_ref[...], 0.0)
        gains_ref[place : place + 1] = jnp.sum(chosen, axis=0, keepdims=True)

    lane = lax.broadcasted_iota(jnp.int32, (1, key_count), 1)
    piece = lane // rows
    place = jnp.where(piece % 2 == head, 0, rows) + lane % rows
    clip = ((piece // 2) % 2 * 2 + piece // 4) ^ ctx
    here = place < pick_out(counts_ref, clip)
    seen = pick_out(visible_ref.at[pl.ds(ctx, 1)], clip) == 1
    bias_ref[:1] = jnp.where(here & seen, 0.0, -1e30)
    bias_ref[1:] = jnp.where(here & (clip == 0), 0.0, -1e30)
    row = lax.broadcasted_iota(jnp.int32, live_ref.shape[1:], 0)
    live_ref[0] = jnp.where(row + head * rows < pick_out(counts_ref, ctx), 1.0, 0.0)
    live_ref[1] = jnp.where(row + ctx * first_rows < pick_out(counts_ref, 0), 1.0, 0.0)


def attend(query_pieces, keys, values, key_bias):
    scale = 1.0 / math.sqrt(HEAD_SIZE)
    stacked = jnp.concatenate(query_pieces, axis=0)
    scores = lax.dot_general(
        stacked, keys, (((1,), (1,)), ((), ())), preferred_element_type=jnp.float32
    )
    scores = scores * scale + key_bias
    peak = jnp.max(scores, axis=1, keepdims=True)
    probs = jnp.exp(scores - peak)
    denominator = jnp.sum(probs, axis=1, keepdims=True)
    weighted = jnp.dot(probs.astype(jnp.bfloat16), values, preferred_element_type=jnp.float32)
    return weighted / denominator


def stage_kernel(query_ref, key_ref, value_ref, small_refs, held_ref, joined_ref, small_held_refs, sems):
    width = key_ref.shape[1]
    sources = (key_ref, value_ref, query_ref, *small_refs)
    targets = (joined_ref.at[:, pl.ds(0, width)], joined_ref.at[:, pl.ds(width, width)], held_ref, *small_held_refs)
    copies = [
        pltpu.make_async_copy(source, target, sems.at[place])
        for place, (source, target) in enumerate(zip(sources, targets))
    ]
    for copy in copies:
        copy.start()
    for copy in copies:
        copy.wait()


def pick_kernel(query_ref, swapped_ref, kept_ref, sent_ref):
    ctx, head = lax.axis_index("ctx"), lax.axis_index("head")
    rows, half = kept_ref.shape

    def hand_on(ref, first):
        for side, (kept, sent) in enumerate(((0, half), (half, 0))):

            @pl.when(head == side)
            def _(kept=kept, sent=sent):
                kept_ref[...] = ref[first : first + rows, kept : kept + half]
                sent_ref[...] = ref[first : first + rows, sent : sent + half]

    @pl.when(ctx % 2 == 0)
    def _():
        hand_on(query_ref, 0)

    @pl.when(ctx % 2 == 1)
    def _():
        hand_on(swapped_ref, rows)


def attention_kernel(
    query_ref,
    first_refs,
    near_refs,
    far_refs,
    bias_ref,
    live_ref,
    gain_ref,
    far_gain_ref,
    mixed_ref,
    finished_ref,
    mixed_blocks,
    finished_block,
    sems,
):
    ctx, head = lax.axis_index("ctx"), lax.axis_index("head")
    rows, width = query_ref.shape
    half = width // 2
    first_rows = finished_ref.shape[0]
    group = QUERY_HEADS // KEY_VALUE_HEADS
    group_width = group * HEAD_SIZE
    kv_width = KEY_VALUE_HEADS * HEAD_SIZE

    def load(kind, first):
        columns = pl.ds(first, HEAD_SIZE)
        joined = pl.ds(pl.multiple_of(kind * kv_width + first, HEAD_SIZE), HEAD_SIZE)
        pieces = [ref[:, joined] for ref in near_refs[:2]]
        pieces += [ref[:, columns] for ref in near_refs[2 + 2 * kind : 4 + 2 * kind]]
        pieces += [ref[:, joined] for ref in far_refs[:2]]
        for part in (2 * kind, 2 * kind + 1):
            pieces.append(far_refs[2][part * rows : (part + 1) * rows, columns])
        return jnp.concatenate(pieces, axis=0)

    live = live_ref[0] != 0.0
    for kv_head in range(KEY_VALUE_HEADS):
        keys, values = load(0, kv_head * HEAD_SIZE), load(1, kv_head * HEAD_SIZE)
        start = kv_head * group_width
        spans = [slice(start + g * HEAD_SIZE, start + (g + 1) * HEAD_SIZE) for g in range(group)]
        queries = [query_ref[:, span] for span in spans]
        attended = attend(queries, keys, values, bias_ref[:1])
        for g, span in enumerate(spans):
            side = span.start // half
            local = slice(span.start - side * half, span.stop - side * half)
            gain = jnp.where(head == side, gain_ref[:1, local], far_gain_ref[:1, local])
            block = attended[g * rows : (g + 1) * rows] * gain
            mixed_blocks[:, span] = jnp.where(live, block, 0.0).astype(mixed_blocks.dtype)
        done = pl.ds(start, group_width)
        pltpu.make_async_copy(mixed_blocks.at[:, done], mixed_ref.at[:, done], sems.at[kv_head]).start()

    kept_ref, turned_ref, across_ref = first_refs
    first_live = live_ref[1, :first_rows] != 0.0
    for kv_head in range(KEY_VALUE_HEADS // 2):
        start = pl.multiple_of((head * (KEY_VALUE_HEADS // 2) + kv_head) * HEAD_SIZE, HEAD_SIZE)
        keys, values = load(0, start), load(1, start)
        start = kv_head * group_width
        spans = [slice(start + g * HEAD_SIZE, start + (g + 1) * HEAD_SIZE) for g in range(group)]
        queries = [
            jnp.where(
                ctx < 2,
                jnp.where(head == 0, kept_ref[:, span], turned_ref[:, span]),
                jnp.where(head == 0, turned_ref[:, span], across_ref[:, span]),
            )
            for span in spans
        ]
        attended = attend(queries, keys, values, bias_ref[1:])
        for g, span in enumerate(spans):
            block = attended[g * first_rows : (g + 1) * first_rows] * gain_ref[1:, span]
            finished_block[:, span] = jnp.where(first_live, block, 0.0).astype(finished_block.dtype)
    last = pltpu.make_async_copy(finished_block, finished_ref, sems.at[KEY_VALUE_HEADS])
    last.start()
    for kv_head in range(KEY_VALUE_HEADS):
        done = pl.ds(kv_head * group_width, group_width)
        pltpu.make_async_copy(mixed_blocks.at[:, done], mixed_ref.at[:, done], sems.at[kv_head]).wait()
    last.wait()


def paired_body(queries, keys, values, level_gain, levels, visible, counts):
    axes = ("ctx", "head")
    places = [(c, h) for c in range(CLIPS) for h in range(2)]
    rows, width = queries.shape
    half = width // 2
    first_rows = rows * 2 // CLIPS

    def move(block, route):
        pairs = [(a * 2 + b, c * 2 + d) for (a, b), (c, d) in route]
        return lax.ppermute(block, axes, pairs)

    beside = [((c, h), (c, 1 - h)) for c, h in places]
    across = [((c, h), (c ^ 2, h)) for c, h in places]
    partner = [((c, h), (c ^ 1, h)) for c, h in places]
    relay = [((c, h), (c, 1 - h) if c >= 2 else (c ^ 1, h)) for c, h in places]
    corner = [((c, h), (c + 2, 1 - h) if c < 2 else (c - 2, h)) for c, h in places]
    up = [((c, h), (c ^ 2, h) if h == 1 else (c ^ 1, h)) for c, h in places]
    turn = [((2, 1), (3, 1)), ((3, 1), (2, 1))]
    for c in range(2):
        turn += [((c, 0), (c, 1)), ((c, 1), (c + 2, 0)), ((c + 2, 0), (c, 0))]
    vmem = pl.BlockSpec(memory_space=pltpu.VMEM)
    anywhere = pl.BlockSpec(memory_space=pl.ANY)
    params = pltpu.CompilerParams(vmem_limit_bytes=KERNEL_BYTES)

    def in_hbm(*arrays):
        return [pltpu.with_memory_space_constraint(array, pltpu.HBM) for array in arrays]

    swapped = move(queries, partner)
    across_values = move(values, across)
    small = [levels[None], visible, counts[None]]
    shapes = [jax.ShapeDtypeStruct(x.shape, x.dtype) for x in (queries, *small)]
    joined_shape = jax.ShapeDtypeStruct((rows, 2 * keys.shape[1]), keys.dtype)
    held, joined, small = pl.pallas_call(
        stage_kernel,
        out_shape=(shapes[0], joined_shape, shapes[1:]),
        in_specs=[anywhere] * 3 + [[anywhere] * 3],
        out_specs=(vmem, vmem, [vmem] * 3),
        scratch_shapes=[pltpu.SemaphoreType.DMA((6,))],
        compiler_params=params,
        name="stage",
    )(*in_hbm(queries, keys, values), in_hbm(*small))
    beside_joined = move(joined, beside)
    across_keys, corner_keys = move(keys, across), move(keys, corner)
    corner_values = move(across_values, relay)
    rest = [across_keys, corner_keys, across_values, corner_values]
    near = [joined, beside_joined, *rest]
    far = [move(joined, partner), move(beside_joined, partner)]
    joined_rest = jnp.concatenate(rest, axis=0)
    far.append(move(joined_rest, partner))

    block = jax.ShapeDtypeStruct((first_rows, half), queries.dtype)
    kept, sent = pl.pallas_call(
        pick_kernel,
        out_shape=(block, block),
        in_specs=[vmem, vmem],
        out_specs=(vmem, vmem),
        compiler_params=params,
        name="pick",
    )(held, swapped)
    turned, raised = move(sent, turn), move(kept, up)

    gains, bias, live = pl.pallas_call(
        prepare_kernel,
        out_shape=(
            jax.ShapeDtypeStruct((2, half), level_gain.dtype),
            jax.ShapeDtypeStruct((2, 2 * CLIPS * rows), jnp.float32),
            jax.ShapeDtypeStruct((2, rows, HEAD_SIZE), jnp.float32),
        ),
        in_specs=[vmem] * 4,
        out_specs=(vmem, vmem, vmem),
        compiler_params=params,
        name="prepare",
    )(*small, level_gain)
    far_gains = move(gains, beside)
    return pl.pallas_call(
        attention_kernel,
        out_shape=(jax.ShapeDtypeStruct((rows, width), queries.dtype), block),
        in_specs=[vmem, [vmem] * 3, [vmem] * 6, [vmem] * 3] + [vmem] * 4,
        out_specs=(anywhere, anywhere),
        scratch_shapes=[
            pltpu.VMEM((rows, width), queries.dtype),
            pltpu.VMEM((first_rows, half), queries.dtype),
            pltpu.SemaphoreType.DMA((KEY_VALUE_HEADS + 1,)),
        ],
        compiler_params=params,
        name="attention",
    )(held, [kept, turned, raised], near, far, bias, live, gains, far_gains)


def solution(mesh):
    placed = (
        P(("dp", "ctx", "head"), None),
        P(("dp", "ctx", "head"), None),
        P(("dp", "ctx", "head"), None),
        P(None, "head"),
        P("dp"),
        P("dp", None),
        P("dp"),
    )
    axes = mesh.shape
    paired = axes["ctx"] == CLIPS and axes["head"] == 2
    return jax.shard_map(
        paired_body if paired else general_body,
        mesh=mesh,
        in_specs=placed,
        out_specs=(P(("dp", "ctx", "head"), None), P(("dp", "ctx"), "head")),
        check_vma=False,
    )
```
